32 devices in a mesh: groups: 2 (over x), view: 16 (over z, y, core).
Axes of the slice: x: 2, y: 2, z: 4, core: 2. Of those that a mesh axis runs over, the one named last changes fastest.
Arguments:
- estimate: float32 [6144, 128], P(('groups', 'view')), parts along dimension 0, may hold values from 0.5 to 2, as said below
- measured: bfloat16 [512, 192, 128], P(('groups', 'view')), parts along dimension 0, may hold values from 0.25 to 4, as said below
- kernel_z: bfloat16 [16, 3, 128, 128], replicated, may hold values from 0 to 2, as said below
- kernel_x: bfloat16 [16, 3, 12, 12], replicated, may hold values from 0 to 2, as said below
- kernel_y: bfloat16 [16, 3, 16, 16], replicated, may hold values from 0 to 2, as said below
- background: bfloat16 [16], replicated, may hold values from 0.049804688 to 0.5
- relax: bfloat16 [16], replicated, may hold values from 0.029907227 to 0.23925781
- owner: int32 [512, 1], P(('groups', 'view')), parts along dimension 0, may hold values from 0 to 15; in each aligned block of 16 rows (0 to 15, 16 to 31, ...) at most 2 rows name the same one
- source_offset: int32 [512], P(('groups', 'view')), parts along dimension 0, may hold values from 0 to 184
- tile_offset: int32 [512], P(('groups', 'view')), parts along dimension 0, may hold values from 0 to 56
- feather: int32 [512, 8], P(('groups', 'view')), parts along dimension 0, may hold values from 1 to 8
Outputs:
- refined: float32 [6144, 128], P(('groups', 'view')), parts along dimension 0
- smoothed: float32 [2048, 128], P(('groups', 'view')), parts along dimension 0
The draws below stay inside these ranges and needn't reach their ends.
There are 2 independent parts, one for each index of `groups`. The reference program is written for one: setup_inputs(seed, part) draws one part's arguments, and reference() takes and returns one part's arrays. A program takes and returns all parts, laid end to end along the dimension named above; an argument that names none is the same for every part. Nothing has to cross between parts.
Inputs may be any that keep to these rules, and one draw needn't show every extreme that they name: `owner`: within the 16 rows of one block no tile is named more than 2 times, and in every draw some tile is named exactly 2 times by some block. `kernel_z`: entries are nonnegative and every diagonal entry is positive. `kernel_x`: entries are nonnegative and every diagonal entry is positive. `kernel_y`: entries are nonnegative and every diagonal entry is positive. `estimate`: entries are positive. `measured`: entries are positive.
All inputs are finite; a program needn't handle non-finite values.
Results may differ from the reference program's by a relative error of at most 0.0006.
Values may be sent and summed in bfloat16 or wider, within the bound.
A program may use at most 64 MiB of HBM per device.

```python
import math
import jax
import jax.numpy as jnp
import numpy as np
from jax import lax

BX = 12
BY = 16
BZ = 128
VIEWS = 16
RANK = 3
SROWS = 8
TROWS = 64
CAP = 2
BLOCKS = 16
ROWS = 192
LIST = 16


def draw_kernel(key, extent):
    key_spread, key_factor = jax.random.split(key)
    spread = jnp.exp(jax.random.uniform(key_spread, (VIEWS, RANK, 1, 1), jnp.float32, jnp.log(0.7), jnp.log(3.0)))
    positions = jnp.arange(extent, dtype=jnp.float32)
    spacing = positions[:, None] - positions[None, :]
    profile = jnp.exp(-spacing * spacing / (2.0 * spread * spread))
    profile = profile / jnp.sum(profile, axis=-1, keepdims=True)
    factor = jax.random.uniform(key_factor, (VIEWS, RANK, extent, extent), jnp.float32, 0.5, 1.5)
    return (0.7 * profile * factor).astype(jnp.bfloat16)


def draw_kernel_z(key, part):
    return draw_kernel(jax.random.fold_in(key, 31), BZ)


def draw_kernel_x(key, part):
    return draw_kernel(jax.random.fold_in(key, 37), BX)


def draw_kernel_y(key, part):
    return draw_kernel(jax.random.fold_in(key, 41), BY)


def draw_estimate(key, part):
    key_rough = jax.random.fold_in(jax.random.fold_in(key, 43), 0)
    rough = jax.random.uniform(key_rough, (BLOCKS * ROWS, BZ), jnp.float32, jnp.log(0.5), jnp.log(2.0))
    values = jnp.exp(rough)
    return jnp.clip(values, 0.5, 2.0).astype(jnp.float32)


def draw_measured(key, part):
    key_rough = jax.random.fold_in(jax.random.fold_in(key, 47), 0)
    rough = jax.random.uniform(key_rough, (BLOCKS * VIEWS, ROWS, BZ), jnp.float32, jnp.log(0.5), jnp.log(2.0))
    values = jnp.exp(rough)
    return jnp.clip(values, 0.25, 4.0).astype(jnp.bfloat16)


def set_ends(result, own_key, least, largest):
    shape = result.shape
    spot = [jax.random.randint(jax.random.fold_in(own_key, axis), (), 0, shape[axis]) for axis in range(len(shape))]
    result = result.at[tuple(spot)].set(least)
    longest = shape.index(max(shape))
    spot[longest] = (spot[longest] + 1) % shape[longest]
    return result.at[tuple(spot)].set(largest)


def assign_block(own_key, own, number, rows, amount, top, reach, slope):
    ranking = jax.random.permutation(own_key, amount)
    crowded, usual = load_shares(amount, rows * top, reach, slope, True), load_shares(amount, rows * top, reach, slope, False)
    places = jnp.arange(amount)

    def named(sizes, offset_by):
        used = int((sizes > 0).sum())
        fixed = max(1, used // 4)
        moved = fixed + (places - fixed + offset_by * (used - fixed)) % max(1, amount - fixed)
        return jnp.zeros((amount,), jnp.int32).at[ranking[jnp.where(places < fixed, places, moved)]].set(jnp.asarray(sizes, jnp.int32))

    sizes = jnp.where(number % 4 == 0, named(crowded, number // 4), named(usual, number - number // 4 - 1))
    mixed = jax.random.permutation(jax.random.fold_in(own, 3), amount)
    donor, receiver = mixed[0:amount // 2 * 2:2], mixed[1:amount // 2 * 2:2]
    room = jnp.minimum(sizes[donor] - 1, reach - sizes[receiver]) // 2
    room = jnp.where((donor == ranking[0]) | (receiver == ranking[0]) | (sizes[receiver] == 0), 0, jnp.maximum(room, 0))
    moved = jax.random.randint(jax.random.fold_in(own, 4), (amount // 2,), 0, 1 << 20) % (room + 1)
    sizes = sizes.at[donor].add(-moved).at[receiver].add(moved)
    items = jnp.searchsorted(jnp.cumsum(sizes), jnp.arange(rows * top), side="right").astype(jnp.int32)
    listing = items.reshape(top, rows).T
    listing = listing[jax.random.permutation(jax.random.fold_in(own, 1), rows)]
    offset_by = jax.random.randint(jax.random.fold_in(own, 2), (rows, 1), 0, top)
    return jnp.take_along_axis(listing, (jnp.arange(top)[None, :] + offset_by) % top, axis=1)


def load_shares(amount, total, bound, slope, full):
    loads = [(1 << 20) // math.isqrt(rank ** slope) + 1 for rank in range(1, amount + 1)]
    largest = bound if full else min(bound, max(-(-total // amount), total * loads[0] // sum(loads)))
    least = 1 if total - largest >= amount - 1 else 0
    counts, spare = [largest] + [least] * (amount - 1), total - largest - least * (amount - 1)
    while spare > 0:
        candidates = [i for i in range(1, amount) if counts[i] < largest] or [i for i in range(1, amount) if counts[i] < bound]
        mass, left = sum([loads[i] for i in candidates]), spare
        for i in candidates:
            addition = min(bound - counts[i], max(1, left * loads[i] // mass), spare)
            counts[i] = counts[i] + addition
            spare = spare - addition
    return np.array(counts)


def setup_inputs(seed: int = 0, part: int = 0) -> dict:
    arg_keys = jax.random.split(jax.random.key(seed), 12)
    part_keys = jax.random.split(jax.random.fold_in(arg_keys[11], part), 12)
    estimate = draw_estimate(jax.random.fold_in(jax.random.fold_in(arg_keys[11], part), 71), part)
    measured = draw_measured(jax.random.fold_in(jax.random.fold_in(arg_keys[11], part), 71), part)
    kernel_z = draw_kernel_z(jax.random.fold_in(arg_keys[11], 71), part)
    kernel_x = draw_kernel_x(jax.random.fold_in(arg_keys[11], 71), part)
    kernel_y = draw_kernel_y(jax.random.fold_in(arg_keys[11], 71), part)
    background = jnp.clip(jnp.exp(jax.random.uniform(arg_keys[5], (VIEWS,), jnp.float32, math.log(0.049804688), math.log(0.5))), 0.049804688, 0.5).astype(jnp.bfloat16)
    relax = jnp.clip(jnp.exp(jax.random.uniform(arg_keys[6], (VIEWS,), jnp.float32, math.log(0.029907227), math.log(0.23925781))), 0.029907227, 0.23925781).astype(jnp.bfloat16)
    owner_keys = jax.random.split(jax.random.fold_in(part_keys[7], 1), (BLOCKS * LIST) // LIST)
    owner_turns = jax.random.permutation(jax.random.fold_in(part_keys[7], 3), (BLOCKS * LIST) // LIST)
    owner = jax.vmap(lambda own, number: assign_block(jax.random.fold_in(part_keys[7], 2), own, number, LIST, BLOCKS, 1, CAP, 2))(owner_keys, owner_turns).reshape((BLOCKS * LIST, 1))
    source_offset = set_ends(jax.random.randint(part_keys[8], (BLOCKS * LIST,), 0, ROWS - SROWS + 1), jax.random.fold_in(part_keys[8], 1), 0, ROWS - SROWS).astype(jnp.int32)
    tile_offset = set_ends(jax.random.randint(part_keys[9], (BLOCKS * LIST,), 0, TROWS - SROWS + 1), jax.random.fold_in(part_keys[9], 1), 0, TROWS - SROWS).astype(jnp.int32)
    feather = set_ends(jax.random.randint(part_keys[10], (BLOCKS * LIST, SROWS), 1, 9), jax.random.fold_in(part_keys[10], 1), 1, 8).astype(jnp.int32)
    return dict(estimate=estimate, measured=measured, kernel_z=kernel_z, kernel_x=kernel_x, kernel_y=kernel_y, background=background, relax=relax, owner=owner, source_offset=source_offset, tile_offset=tile_offset, feather=feather)


smooth_rate = 0.24
edge_scale = 1.0


def kron_rows(kernel_x, kernel_y):
    outer = kernel_x.astype(jnp.float32)[..., :, None, :, None] * kernel_y.astype(jnp.float32)[..., None, :, None, :]
    rows_xy = kernel_x.shape[-1] * kernel_y.shape[-1]
    return outer.reshape(outer.shape[:-4] + (rows_xy, rows_xy)).astype(jnp.bfloat16)


def rounded(values):
    return lax.optimization_barrier(values.astype(jnp.bfloat16)).astype(jnp.float32)


def visit_view(block, kernel_z, kernel_xy, measured_block, back_value, relax_value):
    highest = lax.Precision.HIGHEST
    zeta = kernel_z.astype(jnp.float32)
    plane = kernel_xy.astype(jnp.float32)
    lowered = rounded(block)
    along_z = rounded(jnp.einsum("iz,rkz->rik", lowered, zeta, precision=highest))
    forward = jnp.einsum("rij,rjk->ik", plane, along_z, precision=highest)
    ratio_lo = rounded(measured_block.astype(jnp.float32) / (forward + back_value))
    back_z = rounded(jnp.einsum("ik,rkz->riz", ratio_lo, zeta, precision=highest))
    adjoint = jnp.einsum("rji,rjz->iz", plane, back_z, precision=highest)
    weights_sum = jnp.einsum("ri,rz->iz", jnp.sum(plane, axis=1), jnp.sum(zeta, axis=1), precision=highest)
    return block * jnp.exp(relax_value * jnp.log(adjoint / weights_sum))


def diffuse(volume):
    padded = jnp.pad(volume, 1)
    flux_sum = jnp.zeros_like(volume)
    for neighbor in (padded[2:, 1:-1], padded[:-2, 1:-1], padded[1:-1, 2:], padded[1:-1, :-2]):
        change = neighbor - volume
        flux_sum = flux_sum + change / (1.0 + (change / edge_scale) * (change / edge_scale))
    return volume + smooth_rate * flux_sum


def reference(estimate, measured, kernel_z, kernel_x, kernel_y, background, relax, owner, source_offset, tile_offset, feather):
    blocks = estimate.reshape(BLOCKS, ROWS, BZ)
    measured_all = measured.reshape(BLOCKS, VIEWS, ROWS, BZ)
    kernel_xy = kron_rows(kernel_x, kernel_y)
    back_values = background.astype(jnp.float32)
    relax_values = relax.astype(jnp.float32)

    def run_block(block_id, block):
        def advance(stop_id, carried):
            host_id = (block_id + stop_id) % BLOCKS
            view_id = host_id % VIEWS
            return visit_view(carried, kernel_z[view_id], kernel_xy[view_id], measured_all[host_id, stop_id], back_values[view_id], relax_values[view_id])
        return lax.fori_loop(0, VIEWS, advance, block)

    refined = jax.vmap(run_block)(jnp.arange(BLOCKS, dtype=jnp.int32), blocks).reshape(BLOCKS * ROWS, BZ)
    entries = jnp.arange(BLOCKS * LIST, dtype=jnp.int32)
    window_rows = jnp.arange(SROWS, dtype=jnp.int32)
    source_rows = ((entries // LIST) * ROWS + source_offset)[:, None] + window_rows[None, :]
    target_rows = (owner[:, 0] * TROWS + tile_offset)[:, None] + window_rows[None, :]
    weights = feather.astype(jnp.float32)
    pieces = refined[source_rows] * weights[..., None]
    numerator = 1.0 + jnp.zeros((BLOCKS * TROWS, BZ), jnp.float32).at[target_rows.reshape(-1)].add(pieces.reshape(-1, BZ))
    denominator = 1.0 + jnp.zeros((BLOCKS * TROWS,), jnp.float32).at[target_rows.reshape(-1)].add(weights.reshape(-1))
    joined = numerator / denominator[:, None]
    return refined, diffuse(joined)
```

```python
import functools

import jax
import jax.numpy as jnp
import numpy as np
from jax import lax
from jax.experimental import pallas as pl
from jax.experimental.pallas import tpu as pltpu
from jax.sharding import PartitionSpec as P

CAP = 2
TROWS = 64
smooth_rate = 0.24

f32 = jnp.float32
bf16 = jnp.bfloat16


def split3(x):
    hi = x.astype(bf16)
    rest = x - hi.astype(f32)
    mid = rest.astype(bf16)
    low = (rest - mid.astype(f32)).astype(bf16)
    return hi, mid, low


def onehot_dot(onehot, parts):
    total = None
    for part in reversed(parts):
        term = jnp.dot(onehot, part, preferred_element_type=f32)
        total = term if total is None else total + term
    return total


def kernel(
    nv,
    views,
    bx,
    by,
    srows,
    scal_ref,
    est_ref,
    meas_hbm,
    kz_hbm,
    fac_ref,
    sel_ref,
    owner_ref,
    meta_ref,
    refined_ref,
    smooth_ref,
    rec,
    kz,
    lanes,
    kron,
    logws,
    meta_send,
    meta_recv,
    gather,
    wcol,
    place,
    data_send,
    data_recv,
    joined_ref,
    halo,
    rec_send_sem,
    rec_recv_sem,
    kz_sem,
    meta_send_sem,
    meta_recv_sem,
    data_send_sem,
    data_recv_sem,
    halo_send_sem,
    halo_recv_sem,
):
    me = lax.axis_index("view")
    rows, depth = est_ref.shape
    rank = kz.shape[1]
    listed = owner_ref.shape[0]
    slab = CAP * srows
    landing = nv * slab

    barrier = pltpu.get_barrier_semaphore()

    def greet(d, c):
        pl.semaphore_signal(barrier, inc=1, device_id={"view": lax.rem(me + d, nv)})
        return c

    lax.fori_loop(1, nv, greet, 0)

    own_rec = pltpu.make_async_copy(meas_hbm.at[0], rec.at[0], rec_recv_sem.at[0])
    own_rec.start()
    kz_copy = pltpu.make_async_copy(kz_hbm, kz, kz_sem)
    kz_copy.start()

    def rec_copy(s):
        return pltpu.make_async_remote_copy(
            src_ref=meas_hbm.at[s],
            dst_ref=rec.at[s],
            send_sem=rec_send_sem.at[s],
            recv_sem=rec_recv_sem.at[s],
            device_id={"view": lax.rem(me - s + nv, nv)},
        )

    def peer_copy(src, dst, send_sem, recv_sem, d):
        peer = lax.rem(me + d, nv)
        return pltpu.make_async_remote_copy(
            src_ref=src.at[peer],
            dst_ref=dst.at[me],
            send_sem=send_sem.at[d],
            recv_sem=recv_sem.at[d],
            device_id={"view": peer},
        )

    def meta_copy(d):
        return peer_copy(meta_send, meta_recv, meta_send_sem, meta_recv_sem, d)

    def data_copy(d):
        return peer_copy(data_send, data_recv, data_send_sem, data_recv_sem, d)

    own_col = owner_ref[...].astype(f32)
    own_wide = jnp.broadcast_to(own_col, (listed, 128))
    if listed < 128:
        own_wide = jnp.concatenate([own_wide, jnp.full((128 - listed, 128), -1.0, f32)], axis=0)
    own_row = own_wide.T[0:1, :]
    same = (own_wide == own_row).astype(f32)
    ia = lax.broadcasted_iota(jnp.int32, (128, 128), 0)
    ib = lax.broadcasted_iota(jnp.int32, (128, 128), 1)
    earlier = jnp.where(ia < ib, same, 0.0)
    rank_row = jnp.sum(earlier, axis=0, keepdims=True)
    slot_row = own_row * CAP + rank_row
    slot_of_row = (lax.broadcasted_iota(jnp.int32, (landing, 128), 0) >> 3).astype(f32)
    pick = (slot_of_row == slot_row).astype(f32)[:, :listed].astype(bf16)
    meta = jnp.dot(pick, meta_ref[...].astype(bf16), preferred_element_type=f32)
    meta_send[...] = meta.reshape(nv, slab, 128)

    view0 = lax.rem(me, views)

    def expand(view, slot):
        lanes[...] = jnp.dot(fac_ref[view], sel_ref[...], preferred_element_type=f32)
        for t in range(2):
            base = t * 2 * 16
            y_part = lanes[base + 16 : base + 16 + by, :]
            for x in range(bx):
                x_part = lanes[base + x : base + x + 1, :]
                kron[slot, t, x * by : (x + 1) * by, :] = (x_part * y_part).astype(bf16)

    def weigh(view, slot):
        pieces = []
        for r in range(rank):
            column = jnp.sum(kz[view, r].astype(f32), axis=0, keepdims=True)
            hi = column.astype(bf16).astype(f32)
            both = jnp.concatenate([hi, column - hi], axis=1)
            pieces.append(jnp.broadcast_to(both, (rows, 2 * depth)).astype(bf16))
        halves = jnp.dot(kron[slot, 1], jnp.concatenate(pieces, axis=0), preferred_element_type=f32)
        logws[slot] = jnp.log(halves[:, :depth] + halves[:, depth:])

    expand(view0, 0)
    pl.semaphore_wait(barrier, nv - 1)

    def send_rec(s, c):
        rec_copy(s).start()
        return c

    lax.fori_loop(1, views, send_rec, 0)

    def send_meta(d, c):
        meta_copy(d).start()
        return c

    lax.fori_loop(1, nv, send_meta, 0)

    refined_ref[...] = est_ref[...]
    kz_copy.wait()
    weigh(view0, 0)
    q_of_row = (lax.broadcasted_iota(jnp.int32, (landing, 128), 0) & 7).astype(f32)
    lane_of = lax.broadcasted_iota(jnp.int32, (landing, 128), 1).astype(f32)
    valid = meta[:, 2:3]
    source = meta[:, 0:1] + q_of_row[:, 0:1] + (valid - 1.0) * 4096.0
    lane_rows = lax.broadcasted_iota(jnp.int32, (landing, rows), 1).astype(f32)
    gather[...] = (lane_rows == source).astype(f32).astype(bf16)
    wcol[...] = jnp.broadcast_to(
        jnp.sum(jnp.where(lane_of == q_of_row + 3.0, meta, 0.0), axis=1, keepdims=True), (landing, depth)
    )
    own_rec.wait()

    def stop(s, c):
        @pl.when(s > 0)
        def _():
            rec_copy(s).wait_recv()

        slot = lax.rem(s, 2)
        view = lax.rem(me + s, views)
        e = refined_ref[...]
        zeta = kz[view]
        low = e.astype(bf16)
        along = [
            lax.dot_general(
                low, zeta[r], (((1,), (1,)), ((), ())), preferred_element_type=f32
            ).astype(bf16)
            for r in range(rank)
        ]
        forward = jnp.dot(kron[slot, 0], jnp.concatenate(along, axis=0), preferred_element_type=f32)
        ratio = (rec[s].astype(f32) / (forward + scal_ref[0, view])).astype(bf16)
        back = [
            jnp.dot(ratio, zeta[r], preferred_element_type=f32).astype(bf16) for r in range(rank)
        ]
        adjoint = jnp.dot(kron[slot, 1], jnp.concatenate(back, axis=0), preferred_element_type=f32)
        refined_ref[...] = e * jnp.exp(scal_ref[1, view] * (jnp.log(adjoint) - logws[slot]))
        following = lax.rem(view + 1, views)
        expand(following, 1 - slot)
        weigh(following, 1 - slot)
        return c

    lax.fori_loop(0, views, stop, 0)

    refined = refined_ref[...]
    lines = onehot_dot(gather[...], split3(refined)) * wcol[...]
    data_send[...] = lines.reshape(nv, slab, depth)

    def send_data(d, c):
        data_copy(d).start()
        return c

    lax.fori_loop(1, nv, send_data, 0)
    data_recv[me] = data_send[me]
    meta_recv[me] = meta_send[me]

    def take_meta(d, c):
        meta_copy(d).wait()
        return c

    lax.fori_loop(1, nv, take_meta, 0)

    def done_rec(s, c):
        rec_copy(s).wait_send()
        return c

    lax.fori_loop(1, views, done_rec, 0)

    arrived = meta_recv[...].reshape(landing, 128)
    target = arrived[:, 1:2] + q_of_row[:, 0:1] + (arrived[:, 2:3] - 1.0) * 4096.0
    place_t = (lane_of == target).astype(f32)
    placed = place_t.T[0:TROWS, :].astype(bf16)
    weights = jnp.sum(jnp.where(lane_of == q_of_row + 3.0, arrived, 0.0), axis=1, keepdims=True)
    counted = jnp.dot(
        placed, jnp.broadcast_to(weights, (landing, depth)).astype(bf16), preferred_element_type=f32
    )

    def take_data(d, c):
        data_copy(d).wait()
        return c

    lax.fori_loop(1, nv, take_data, 0)
    summed = onehot_dot(placed, split3(data_recv[...].reshape(landing, depth)))
    joined = (1.0 + summed) / (1.0 + counted)
    joined_ref[...] = joined

    up_copy = pltpu.make_async_remote_copy(
        src_ref=joined_ref.at[pl.ds(TROWS - 8, 8)],
        dst_ref=halo.at[0],
        send_sem=halo_send_sem.at[0],
        recv_sem=halo_recv_sem.at[0],
        device_id={"view": lax.rem(me + 1, nv)},
    )
    down_copy = pltpu.make_async_remote_copy(
        src_ref=joined_ref.at[pl.ds(0, 8)],
        dst_ref=halo.at[1],
        send_sem=halo_send_sem.at[1],
        recv_sem=halo_recv_sem.at[1],
        device_id={"view": lax.rem(me - 1 + nv, nv)},
    )
    up_copy.start()
    down_copy.start()

    lane = lax.broadcasted_iota(jnp.int32, (TROWS, depth), 1)
    line = lax.broadcasted_iota(jnp.int32, (TROWS, depth), 0)

    def flux(neighbor):
        change = neighbor - joined
        return change / (1.0 + change * change)

    right = jnp.where(lane == depth - 1, 0.0, pltpu.roll(joined, depth - 1, 1))
    left = jnp.where(lane == 0, 0.0, pltpu.roll(joined, 1, 1))
    along_depth = flux(right) + flux(left)
    after = pltpu.roll(joined, TROWS - 1, 0)
    before = pltpu.roll(joined, 1, 0)
    up_copy.wait()
    down_copy.wait()
    has_low = (me > 0).astype(f32)
    has_high = (me < nv - 1).astype(f32)
    low_line = halo[0, 7:8, :] * has_low
    high_line = halo[1, 0:1, :] * has_high
    after = jnp.where(line == TROWS - 1, high_line, after)
    before = jnp.where(line == 0, low_line, before)
    smooth_ref[...] = joined + smooth_rate * (flux(after) + flux(before) + along_depth)


def on_device(
    estimate,
    measured,
    kernel_z,
    kernel_x,
    kernel_y,
    background,
    relax,
    owner,
    source_offset,
    tile_offset,
    feather,
):
    nv = lax.axis_size("view")
    views, rank, bx, _ = kernel_x.shape
    by = kernel_y.shape[-1]
    rows, depth = estimate.shape
    srows = feather.shape[1]
    listed = owner.shape[0]
    slab = CAP * srows
    landing = nv * slab

    scal = jnp.stack([background.astype(f32), relax.astype(f32)])

    def facts(factor, extent, before, after):
        both = jnp.stack(
            [factor.transpose(0, 2, 1, 3), factor.transpose(0, 3, 1, 2)], axis=1
        ).reshape(views, 2, extent, rank * extent)
        return jnp.pad(both, ((0, 0), (0, 0), (0, 16 - extent), (before, after)))

    fac = jnp.stack(
        [facts(kernel_x, bx, 0, rank * by), facts(kernel_y, by, rank * bx, 0)], axis=2
    ).reshape(views, 64, rank * (bx + by))
    col = np.arange(rank * rows)
    sel_x = col[None, :] // by == np.arange(rank * bx)[:, None]
    sel_y = (col // rows * by + col % by)[None, :] == np.arange(rank * by)[:, None]
    sel = jnp.asarray(np.concatenate([sel_x, sel_y]).astype(np.float32), bf16)
    meta = jnp.concatenate(
        [
            source_offset[:, None],
            tile_offset[:, None],
            jnp.ones((listed, 1), jnp.int32),
            feather,
            jnp.zeros((listed, 128 - 3 - srows), jnp.int32),
        ],
        axis=1,
    ).astype(f32)

    vmem = pl.BlockSpec(memory_space=pltpu.VMEM)
    anym = pl.BlockSpec(memory_space=pl.ANY)
    dma = pltpu.SemaphoreType.DMA
    return pl.pallas_call(
        functools.partial(kernel, nv, views, bx, by, srows),
        out_shape=(
            jax.ShapeDtypeStruct((rows, depth), f32),
            jax.ShapeDtypeStruct((TROWS, depth), f32),
        ),
        in_specs=[
            pl.BlockSpec(memory_space=pltpu.SMEM),
            vmem,
            anym,
            anym,
            vmem,
            vmem,
            vmem,
            vmem,
        ],
        out_specs=(vmem, vmem),
        scratch_shapes=[
            pltpu.VMEM((views, rows, depth), bf16),
            pltpu.VMEM(kernel_z.shape, bf16),
            pltpu.VMEM((64, rank * rows), f32),
            pltpu.VMEM((2, 2, rows, rank * rows), bf16),
            pltpu.VMEM((2, rows, depth), f32),
            pltpu.VMEM((nv, slab, 128), f32),
            pltpu.VMEM((nv, slab, 128), f32),
            pltpu.VMEM((landing, rows), bf16),
            pltpu.VMEM((landing, depth), f32),
            pltpu.VMEM((TROWS, landing), bf16),
            pltpu.VMEM((nv, slab, depth), f32),
            pltpu.VMEM((nv, slab, depth), f32),
            pltpu.VMEM((TROWS, depth), f32),
            pltpu.VMEM((2, 8, depth), f32),
            dma((views,)),
            dma((views,)),
            dma,
            dma((nv,)),
            dma((nv,)),
            dma((nv,)),
            dma((nv,)),
            dma((2,)),
            dma((2,)),
        ],
        compiler_params=pltpu.CompilerParams(collective_id=0, has_side_effects=True),
    )(scal, estimate, measured, kernel_z, fac, sel, owner, meta)


def solution(mesh):
    return jax.shard_map(
        on_device,
        mesh=mesh,
        in_specs=(
            P(("groups", "view"), None),
            P(("groups", "view"), None, None),
            P(),
            P(),
            P(),
            P(),
            P(),
            P(("groups", "view"), None),
            P(("groups", "view")),
            P(("groups", "view")),
            P(("groups", "view"), None),
        ),
        out_specs=(P(("groups", "view"), None), P(("groups", "view"), None)),
        check_vma=False,
    )
```

```python
import functools

import jax
import jax.numpy as jnp
import numpy as np
from jax import lax
from jax.experimental import pallas as pl
from jax.experimental.pallas import tpu as pltpu
from jax.sharding import PartitionSpec as P

CAP = 2
FIELDS = 16
TROWS = 64
smooth_rate = 0.24

f32 = jnp.float32
bf16 = jnp.bfloat16


def split3(x):
    hi = x.astype(bf16)
    rest = x - hi.astype(f32)
    mid = rest.astype(bf16)
    low = (rest - mid.astype(f32)).astype(bf16)
    return hi, mid, low


def onehot_dot(onehot, parts):
    total = None
    for part in reversed(parts):
        term = jnp.dot(onehot, part, preferred_element_type=f32)
        total = term if total is None else total + term
    return total


def kernel(
    nv,
    views,
    bx,
    by,
    srows,
    est_ref,
    meas_hbm,
    kz_hbm,
    kx_ref,
    ky_ref,
    sel_x_ref,
    sel_y_ref,
    back_ref,
    relax_ref,
    owner_ref,
    source_ref,
    tile_ref,
    feather_ref,
    refined_ref,
    smooth_ref,
    rec,
    kz,
    lanes_x,
    lanes_y,
    kron,
    kron_t,
    logws,
    meta_send,
    meta_recv,
    gather,
    wcol,
    data_send,
    data_recv,
    joined_ref,
    halo,
    rec_send_sem,
    rec_recv_sem,
    kz_sem,
    meta_send_sem,
    meta_recv_sem,
    data_send_sem,
    data_recv_sem,
    halo_send_sem,
    halo_recv_sem,
):
    me = lax.axis_index("view")
    rows, depth = est_ref.shape
    rank = kz.shape[1]
    listed = owner_ref.shape[1]
    slab = CAP * srows
    landing = nv * slab

    barrier = pltpu.get_barrier_semaphore()

    def greet(d, c):
        pl.semaphore_signal(barrier, inc=1, device_id={"view": lax.rem(me + d, nv)})
        return c

    lax.fori_loop(1, nv, greet, 0)

    own_rec = pltpu.make_async_copy(meas_hbm.at[0], rec.at[0], rec_recv_sem.at[0])
    own_rec.start()
    kz_copy = pltpu.make_async_copy(kz_hbm, kz, kz_sem)
    kz_copy.start()

    def rec_copy(s):
        return pltpu.make_async_remote_copy(
            src_ref=meas_hbm.at[s],
            dst_ref=rec.at[s],
            send_sem=rec_send_sem.at[s],
            recv_sem=rec_recv_sem.at[s],
            device_id={"view": lax.rem(me - s + nv, nv)},
        )

    def peer_copy(src, dst, send_sem, recv_sem, d):
        peer = lax.rem(me + d, nv)
        return pltpu.make_async_remote_copy(
            src_ref=src.at[peer],
            dst_ref=dst.at[me],
            send_sem=send_sem.at[d],
            recv_sem=recv_sem.at[d],
            device_id={"view": peer},
        )

    def meta_copy(d):
        return peer_copy(meta_send, meta_recv, meta_send_sem, meta_recv_sem, d)

    def data_copy(d):
        return peer_copy(data_send, data_recv, data_send_sem, data_recv_sem, d)

    pl.semaphore_wait(barrier, nv - 1)

    def send_rec(s, c):
        rec_copy(s).start()
        return c

    lax.fori_loop(1, views, send_rec, 0)

    spread_x = spread_y = None
    for r in range(rank):
        part_x = jnp.dot(kx_ref[r].reshape(bx * views, bx), sel_x_ref[r], preferred_element_type=f32)
        part_y = jnp.dot(ky_ref[:, r].reshape(views * by, by), sel_y_ref[r], preferred_element_type=f32)
        spread_x = part_x if spread_x is None else spread_x + part_x
        spread_y = part_y if spread_y is None else spread_y + part_y
    lanes_x[...] = spread_x
    lanes_y[...] = spread_y

    own_row = owner_ref[...].astype(f32)
    if listed < 128:
        own_row = jnp.concatenate([own_row, jnp.full((1, 128 - listed), -1.0, f32)], axis=1)
    own_wide = jnp.broadcast_to(own_row, (128, 128)).T
    same = (own_wide == own_row).astype(f32)
    ia = lax.broadcasted_iota(jnp.int32, (128, 128), 0)
    ib = lax.broadcasted_iota(jnp.int32, (128, 128), 1)
    earlier = jnp.where(ia < ib, same, 0.0)
    rank_row = jnp.sum(earlier, axis=0, keepdims=True)
    slot_row = own_row * CAP + rank_row
    fields = jnp.concatenate(
        [
            source_ref[...].astype(f32),
            tile_ref[...].astype(f32),
            jnp.ones((1, listed), f32),
            feather_ref[...].astype(f32),
            jnp.zeros((FIELDS - 3 - srows, listed), f32),
        ],
        axis=0,
    ).astype(bf16)
    slot_ids = lax.broadcasted_iota(jnp.int32, (nv, 128), 0).astype(f32) * CAP
    facts = []
    for c in range(CAP):
        pick = (slot_ids + c == slot_row).astype(f32)[:, :listed].astype(bf16)
        facts.append(
            lax.dot_general(pick, fields, (((1,), (1,)), ((), ())), preferred_element_type=f32)
        )
    facts.append(jnp.zeros((nv, 128 - CAP * FIELDS), f32))
    facts = jnp.concatenate(facts, axis=1)
    meta_send[...] = facts.reshape(nv, 1, 128)

    def send_meta(d, c):
        meta_copy(d).start()
        return c

    lax.fori_loop(1, nv, send_meta, 0)

    row_id = lax.broadcasted_iota(jnp.int32, (landing, 128), 0)
    lane_of = lax.broadcasted_iota(jnp.int32, (landing, 128), 1)
    q_of_row = lax.rem(row_id, srows)
    first_lane = lax.rem(row_id, slab) // srows * FIELDS
    spread_rows = (
        lax.broadcasted_iota(jnp.int32, (landing, nv), 0) // slab
        == lax.broadcasted_iota(jnp.int32, (landing, nv), 1)
    ).astype(f32).astype(bf16)

    def landing_facts(table, line_lane):
        wide = jnp.dot(spread_rows, table.astype(bf16), preferred_element_type=f32)

        def column(lane):
            return jnp.sum(jnp.where(lane_of == lane, wide, 0.0), axis=1, keepdims=True)

        line = column(first_lane + line_lane) + q_of_row[:, 0:1].astype(f32)
        return line + (column(first_lane + 2) - 1.0) * 4096.0, column(first_lane + 3 + q_of_row)

    view0 = lax.rem(me, views)

    def expand(view, slot):
        y_part = lanes_y[pl.ds(pl.multiple_of(view * by, by), by), :]
        for x in range(bx):
            x_part = lanes_x[pl.ds(x * views + view, 1), :]
            kron[slot, x * by : (x + 1) * by, :] = (x_part * y_part).astype(bf16)

    def weigh(view, slot):
        kron_t[slot] = kron[slot].T
        halves = None
        for r in range(rank):
            column = jnp.sum(kz[view, r].astype(f32), axis=0, keepdims=True)
            hi = column.astype(bf16).astype(f32)
            both = jnp.concatenate([hi, column - hi], axis=1)
            both = jnp.broadcast_to(both, (rows, 2 * depth)).astype(bf16)
            part = jnp.dot(
                kron_t[slot, r * rows : (r + 1) * rows, :], both, preferred_element_type=f32
            )
            halves = part if halves is None else halves + part
        logws[slot] = jnp.log(halves[:, :depth] + halves[:, depth:])

    def scalar(ref, view):
        lane = lax.broadcasted_iota(jnp.int32, (1, views), 1)
        return jnp.sum(jnp.where(lane == view, ref[...].astype(f32), 0.0), axis=1, keepdims=True)

    expand(view0, 0)
    refined_ref[...] = est_ref[...]
    kz_copy.wait()
    weigh(view0, 0)
    source, weight = landing_facts(facts, 0)
    lane_rows = lax.broadcasted_iota(jnp.int32, (landing, rows), 1).astype(f32)
    gather[...] = (lane_rows == source).astype(f32).astype(bf16)
    wcol[...] = jnp.broadcast_to(weight, (landing, depth))
    own_rec.wait()

    def stop(s, c):
        @pl.when(s > 0)
        def _():
            rec_copy(s).wait_recv()

        slot = lax.rem(s, 2)
        view = lax.rem(me + s, views)
        e = refined_ref[...]
        zeta = kz[view]
        low = e.astype(bf16)
        along = [
            lax.dot_general(
                low, zeta[r], (((1,), (1,)), ((), ())), preferred_element_type=f32
            ).astype(bf16)
            for r in range(rank)
        ]
        forward = jnp.dot(kron[slot], jnp.concatenate(along, axis=0), preferred_element_type=f32)
        ratio = (rec[s].astype(f32) / (forward + scalar(back_ref, view))).astype(bf16)
        back = [
            jnp.dot(ratio, zeta[r], preferred_element_type=f32).astype(bf16) for r in range(rank)
        ]
        adjoint = None
        for r in range(rank):
            part = jnp.dot(
                kron_t[slot, r * rows : (r + 1) * rows, :], back[r], preferred_element_type=f32
            )
            adjoint = part if adjoint is None else adjoint + part
        refined_ref[...] = e * jnp.exp(scalar(relax_ref, view) * (jnp.log(adjoint) - logws[slot]))
        following = lax.rem(view + 1, views)
        expand(following, 1 - slot)
        weigh(following, 1 - slot)
        return c

    lax.fori_loop(0, views, stop, 0)

    refined = refined_ref[...]
    lines = onehot_dot(gather[...], split3(refined)) * wcol[...]
    data_send[...] = lines.reshape(nv, slab, depth)

    def send_data(d, c):
        data_copy(d).start()
        return c

    lax.fori_loop(1, nv, send_data, 0)
    data_recv[me] = data_send[me]
    meta_recv[me] = meta_send[me]

    def take_meta(d, c):
        meta_copy(d).wait()
        return c

    lax.fori_loop(1, nv, take_meta, 0)

    def done_rec(s, c):
        rec_copy(s).wait_send()
        return c

    lax.fori_loop(1, views, done_rec, 0)

    target, weights = landing_facts(meta_recv[...].reshape(nv, 128), 1)
    place_t = (lane_of.astype(f32) == target).astype(f32)
    placed = place_t.T[0:TROWS, :].astype(bf16)
    counted = jnp.dot(
        placed, jnp.broadcast_to(weights, (landing, depth)).astype(bf16), preferred_element_type=f32
    )

    def take_data(d, c):
        data_copy(d).wait()
        return c

    lax.fori_loop(1, nv, take_data, 0)
    summed = onehot_dot(placed, split3(data_recv[...].reshape(landing, depth)))
    joined = (1.0 + summed) / (1.0 + counted)
    joined_ref[...] = joined

    up_copy = pltpu.make_async_remote_copy(
        src_ref=joined_ref.at[pl.ds(TROWS - 8, 8)],
        dst_ref=halo.at[0],
        send_sem=halo_send_sem.at[0],
        recv_sem=halo_recv_sem.at[0],
        device_id={"view": lax.rem(me + 1, nv)},
    )
    down_copy = pltpu.make_async_remote_copy(
        src_ref=joined_ref.at[pl.ds(0, 8)],
        dst_ref=halo.at[1],
        send_sem=halo_send_sem.at[1],
        recv_sem=halo_recv_sem.at[1],
        device_id={"view": lax.rem(me - 1 + nv, nv)},
    )
    up_copy.start()
    down_copy.start()

    lane = lax.broadcasted_iota(jnp.int32, (TROWS, depth), 1)
    line = lax.broadcasted_iota(jnp.int32, (TROWS, depth), 0)

    def flux(neighbor):
        change = neighbor - joined
        return change / (1.0 + change * change)

    right = jnp.where(lane == depth - 1, 0.0, pltpu.roll(joined, depth - 1, 1))
    left = jnp.where(lane == 0, 0.0, pltpu.roll(joined, 1, 1))
    along_depth = flux(right) + flux(left)
    after = pltpu.roll(joined, TROWS - 1, 0)
    before = pltpu.roll(joined, 1, 0)
    up_copy.wait()
    down_copy.wait()
    has_low = (me > 0).astype(f32)
    has_high = (me < nv - 1).astype(f32)
    low_line = halo[0, 7:8, :] * has_low
    high_line = halo[1, 0:1, :] * has_high
    after = jnp.where(line == TROWS - 1, high_line, after)
    before = jnp.where(line == 0, low_line, before)
    smooth_ref[...] = joined + smooth_rate * (flux(after) + flux(before) + along_depth)


def on_device(
    estimate,
    measured,
    kernel_z,
    kernel_x,
    kernel_y,
    background,
    relax,
    owner,
    source_offset,
    tile_offset,
    feather,
):
    nv = lax.axis_size("view")
    views, rank, bx, _ = kernel_x.shape
    by = kernel_y.shape[-1]
    rows, depth = estimate.shape
    srows = feather.shape[1]
    listed = owner.shape[0]
    slab = CAP * srows
    landing = nv * slab

    col = np.arange(rank * rows)
    sel_x = col[None, :] // by == np.arange(rank * bx)[:, None]
    sel_y = (col // rows * by + col % by)[None, :] == np.arange(rank * by)[:, None]
    sel_x = jnp.asarray(sel_x.reshape(rank, bx, -1).astype(np.float32), bf16)
    sel_y = jnp.asarray(sel_y.reshape(rank, by, -1).astype(np.float32), bf16)

    vmem = pl.BlockSpec(memory_space=pltpu.VMEM)
    anym = pl.BlockSpec(memory_space=pl.ANY)
    dma = pltpu.SemaphoreType.DMA
    return pl.pallas_call(
        functools.partial(kernel, nv, views, bx, by, srows),
        out_shape=(
            jax.ShapeDtypeStruct((rows, depth), f32),
            jax.ShapeDtypeStruct((TROWS, depth), f32),
        ),
        in_specs=[vmem, anym, anym] + [vmem] * 10,
        out_specs=(vmem, vmem),
        scratch_shapes=[
            pltpu.VMEM((views, rows, depth), bf16),
            pltpu.VMEM(kernel_z.shape, bf16),
            pltpu.VMEM((bx * views, rank * rows), f32),
            pltpu.VMEM((views * by, rank * rows), f32),
            pltpu.VMEM((2, rows, rank * rows), bf16),
            pltpu.VMEM((2, rank * rows, rows), bf16),
            pltpu.VMEM((2, rows, depth), f32),
            pltpu.VMEM((nv, 1, 128), f32),
            pltpu.VMEM((nv, 1, 128), f32),
            pltpu.VMEM((landing, rows), bf16),
            pltpu.VMEM((landing, depth), f32),
            pltpu.VMEM((nv, slab, depth), f32),
            pltpu.VMEM((nv, slab, depth), f32),
            pltpu.VMEM((TROWS, depth), f32),
            pltpu.VMEM((2, 8, depth), f32),
            dma((views,)),
            dma((views,)),
            dma,
            dma((nv,)),
            dma((nv,)),
            dma((nv,)),
            dma((nv,)),
            dma((2,)),
            dma((2,)),
        ],
        compiler_params=pltpu.CompilerParams(collective_id=0, has_side_effects=True),
    )(
        estimate,
        measured,
        kernel_z,
        kernel_x.transpose(1, 2, 0, 3),
        kernel_y,
        sel_x,
        sel_y,
        background.reshape(1, views),
        relax.reshape(1, views),
        owner.reshape(1, listed),
        source_offset.reshape(1, listed),
        tile_offset.reshape(1, listed),
        feather.T,
    )


def solution(mesh):
    return jax.shard_map(
        on_device,
        mesh=mesh,
        in_specs=(
            P(("groups", "view"), None),
            P(("groups", "view"), None, None),
            P(),
            P(),
            P(),
            P(),
            P(),
            P(("groups", "view"), None),
            P(("groups", "view")),
            P(("groups", "view")),
            P(("groups", "view"), None),
        ),
        out_specs=(P(("groups", "view"), None), P(("groups", "view"), None)),
        check_vma=False,
    )
```

```python
import functools

import jax
import jax.numpy as jnp
import numpy as np
from jax import lax
from jax.experimental import pallas as pl
from jax.experimental.pallas import tpu as pltpu
from jax.sharding import PartitionSpec as P

CAP = 2
FIELDS = 16
EDGE = 8
AHEAD = 4
TROWS = 64
smooth_rate = 0.24

f32 = jnp.float32
bf16 = jnp.bfloat16


def split3(x):
    hi = x.astype(bf16)
    rest = x - hi.astype(f32)
    mid = rest.astype(bf16)
    low = (rest - mid.astype(f32)).astype(bf16)
    return hi, mid, low


def onehot_dot(onehot, parts):
    total = None
    for part in reversed(parts):
        term = jnp.dot(onehot, part, preferred_element_type=f32)
        total = term if total is None else total + term
    return total


def kernel(
    nv,
    views,
    bx,
    by,
    srows,
    est_ref,
    meas_hbm,
    kz_hbm,
    kx_ref,
    ky_ref,
    sel_x_ref,
    sel_y_ref,
    back_ref,
    relax_ref,
    owner_ref,
    source_ref,
    tile_ref,
    feather_ref,
    refined_ref,
    smooth_ref,
    rec,
    kz,
    lanes_x,
    lanes_y,
    kron,
    kron_t,
    logws,
    meta_send,
    meta_recv,
    gather,
    edge_lines,
    edge_counts,
    data_send,
    data_recv,
    rec_send_sem,
    rec_recv_sem,
    kz_sem,
    meta_send_sem,
    meta_recv_sem,
    data_send_sem,
    data_recv_sem,
):
    me = lax.axis_index("view")
    rows, depth = est_ref.shape
    rank = kz.shape[1]
    listed = owner_ref.shape[1]
    slab = CAP * srows
    landing = nv * slab

    barrier = pltpu.get_barrier_semaphore()

    def greet(d, c):
        pl.semaphore_signal(barrier, inc=1, device_id={"view": lax.rem(me + d, nv)})
        return c

    lax.fori_loop(1, nv, greet, 0)

    own_rec = pltpu.make_async_copy(meas_hbm.at[0], rec.at[0], rec_recv_sem.at[0])
    own_rec.start()
    kz_copy = pltpu.make_async_copy(kz_hbm, kz, kz_sem)
    kz_copy.start()

    def rec_copy(s):
        return pltpu.make_async_remote_copy(
            src_ref=meas_hbm.at[s],
            dst_ref=rec.at[s],
            send_sem=rec_send_sem.at[s],
            recv_sem=rec_recv_sem.at[s],
            device_id={"view": lax.rem(me - s + nv, nv)},
        )

    def peer_copy(src, dst, send_sem, recv_sem, d):
        peer = lax.rem(me + d, nv)
        return pltpu.make_async_remote_copy(
            src_ref=src.at[peer],
            dst_ref=dst.at[me],
            send_sem=send_sem.at[d],
            recv_sem=recv_sem.at[d],
            device_id={"view": peer},
        )

    def meta_copy(d):
        return peer_copy(meta_send, meta_recv, meta_send_sem, meta_recv_sem, d)

    def data_copy(d):
        return peer_copy(data_send, data_recv, data_send_sem, data_recv_sem, d)

    pl.semaphore_wait(barrier, nv - 1)

    def send_rec(s, c):
        rec_copy(s).start()
        return c

    lax.fori_loop(1, AHEAD, send_rec, 0)

    spread_x = spread_y = None
    for r in range(rank):
        part_x = jnp.dot(kx_ref[r].reshape(bx * views, bx), sel_x_ref[r], preferred_element_type=f32)
        part_y = jnp.dot(ky_ref[:, r].reshape(views * by, by), sel_y_ref[r], preferred_element_type=f32)
        spread_x = part_x if spread_x is None else spread_x + part_x
        spread_y = part_y if spread_y is None else spread_y + part_y
    lanes_x[...] = spread_x
    lanes_y[...] = spread_y

    own_row = owner_ref[...].astype(f32)
    if listed < 128:
        own_row = jnp.concatenate([own_row, jnp.full((1, 128 - listed), -1.0, f32)], axis=1)
    own_wide = jnp.broadcast_to(own_row, (128, 128)).T
    same = (own_wide == own_row).astype(f32)
    ia = lax.broadcasted_iota(jnp.int32, (128, 128), 0)
    ib = lax.broadcasted_iota(jnp.int32, (128, 128), 1)
    earlier = jnp.where(ia < ib, same, 0.0)
    rank_row = jnp.sum(earlier, axis=0, keepdims=True)
    slot_row = own_row * CAP + rank_row
    fields = jnp.concatenate(
        [
            source_ref[...].astype(f32),
            tile_ref[...].astype(f32),
            jnp.ones((1, listed), f32),
            feather_ref[...].astype(f32),
            jnp.zeros((FIELDS - 3 - srows, listed), f32),
        ],
        axis=0,
    ).astype(bf16)
    slot_ids = lax.broadcasted_iota(jnp.int32, (nv, 128), 0).astype(f32) * CAP
    facts = []
    for c in range(CAP):
        pick = (slot_ids + c == slot_row).astype(f32)[:, :listed].astype(bf16)
        facts.append(
            lax.dot_general(pick, fields, (((1,), (1,)), ((), ())), preferred_element_type=f32)
        )
    facts.append(jnp.zeros((nv, 128 - CAP * FIELDS), f32))
    facts = jnp.concatenate(facts, axis=1)
    meta_send[...] = facts.reshape(nv, 1, 128)

    def send_meta(d, c):
        meta_copy(d).start()
        return c

    lax.fori_loop(1, nv, send_meta, 0)

    row_id = lax.broadcasted_iota(jnp.int32, (landing, 128), 0)
    lane_of = lax.broadcasted_iota(jnp.int32, (landing, 128), 1)
    q_of_row = lax.rem(row_id, srows)
    first_lane = lax.rem(row_id, slab) // srows * FIELDS
    spread_rows = (
        lax.broadcasted_iota(jnp.int32, (landing, nv), 0) // slab
        == lax.broadcasted_iota(jnp.int32, (landing, nv), 1)
    ).astype(f32).astype(bf16)

    def landing_facts(table, line_lane):
        wide = jnp.dot(spread_rows, table.astype(bf16), preferred_element_type=f32)

        def column(lane):
            return jnp.sum(jnp.where(lane_of == lane, wide, 0.0), axis=1, keepdims=True)

        line = column(first_lane + line_lane) + q_of_row[:, 0:1].astype(f32)
        return line + (column(first_lane + 2) - 1.0) * 4096.0, column(first_lane + 3 + q_of_row)

    view0 = lax.rem(me, views)

    def expand(view, slot):
        y_part = lanes_y[pl.ds(pl.multiple_of(view * by, by), by), :]
        for x in range(bx):
            x_part = lanes_x[pl.ds(x * views + view, 1), :]
            kron[slot, x * by : (x + 1) * by, :] = (x_part * y_part).astype(bf16)

    def weigh(view, slot):
        kron_t[slot] = kron[slot].T
        halves = None
        for r in range(rank):
            column = jnp.sum(kz[view, r].astype(f32), axis=0, keepdims=True)
            hi = column.astype(bf16).astype(f32)
            both = jnp.concatenate([hi, column - hi], axis=1)
            both = jnp.broadcast_to(both, (rows, 2 * depth)).astype(bf16)
            part = jnp.dot(
                kron_t[slot, r * rows : (r + 1) * rows, :], both, preferred_element_type=f32
            )
            halves = part if halves is None else halves + part
        logws[slot] = jnp.log(halves[:, :depth] + halves[:, depth:])

    def scalar(ref, view):
        lane = lax.broadcasted_iota(jnp.int32, (1, views), 1)
        return jnp.sum(jnp.where(lane == view, ref[...].astype(f32), 0.0), axis=1, keepdims=True)

    expand(view0, 0)
    refined_ref[...] = est_ref[...]
    kz_copy.wait()
    weigh(view0, 0)
    source, weight = landing_facts(facts, 0)
    target, _ = landing_facts(facts, 1)
    lane_rows = lax.broadcasted_iota(jnp.int32, (landing, rows), 1).astype(f32)
    weighted = jnp.where(lane_rows == source, weight, 0.0).astype(bf16)
    gather[...] = weighted
    target_row = jnp.broadcast_to(target, (landing, 128)).T[0:1, :]
    edge_row = lax.broadcasted_iota(jnp.int32, (nv * EDGE, landing), 0)
    edge_kind = lax.rem(edge_row, EDGE)
    side = lax.rem(edge_kind, 2)
    wanted = edge_row // EDGE + 2 * side - 1
    lane_tile = lax.broadcasted_iota(jnp.int32, (nv * EDGE, landing), 1) // slab
    near = jnp.where(side == 0, float(TROWS - 1), 0.0)
    member = ((lane_tile == wanted).astype(f32) * (target_row == near).astype(f32)).astype(bf16)
    kind = lax.rem(lax.broadcasted_iota(jnp.int32, (nv * EDGE, 1), 0), EDGE)
    from_lines = jnp.dot(member, weighted, preferred_element_type=f32)
    edge_lines[...] = jnp.where(kind < 2, from_lines, 0.0).astype(bf16)
    from_weights = jnp.dot(
        member, jnp.broadcast_to(weight, (landing, depth)).astype(bf16), preferred_element_type=f32
    )
    edge_counts[...] = jnp.where((kind >= 2) & (kind < 4), from_weights, 0.0)
    own_rec.wait()

    def stop(s, c):
        @pl.when(s > 0)
        def _():
            rec_copy(s).wait_recv()

        @pl.when(s + AHEAD < views)
        def _():
            rec_copy(s + AHEAD).start()

        slot = lax.rem(s, 2)
        view = lax.rem(me + s, views)
        e = refined_ref[...]
        zeta = kz[view]
        low = e.astype(bf16)
        along = [
            lax.dot_general(
                low, zeta[r], (((1,), (1,)), ((), ())), preferred_element_type=f32
            ).astype(bf16)
            for r in range(rank)
        ]
        forward = jnp.dot(kron[slot], jnp.concatenate(along, axis=0), preferred_element_type=f32)
        ratio = (rec[s].astype(f32) / (forward + scalar(back_ref, view))).astype(bf16)
        back = [
            jnp.dot(ratio, zeta[r], preferred_element_type=f32).astype(bf16) for r in range(rank)
        ]
        adjoint = None
        for r in range(rank):
            part = jnp.dot(
                kron_t[slot, r * rows : (r + 1) * rows, :], back[r], preferred_element_type=f32
            )
            adjoint = part if adjoint is None else adjoint + part
        refined_ref[...] = e * jnp.exp(scalar(relax_ref, view) * (jnp.log(adjoint) - logws[slot]))
        following = lax.rem(view + 1, views)
        expand(following, 1 - slot)
        weigh(following, 1 - slot)
        return c

    lax.fori_loop(0, views, stop, 0)

    parts = split3(refined_ref[...])
    data_send[:, :slab, :] = onehot_dot(gather[...], parts).reshape(nv, slab, depth)
    data_send[:, slab:, :] = (onehot_dot(edge_lines[...], parts) + edge_counts[...]).reshape(
        nv, EDGE, depth
    )

    def send_data(d, c):
        data_copy(d).start()
        return c

    lax.fori_loop(1, nv, send_data, 0)
    data_recv[me] = data_send[me]
    meta_recv[me] = meta_send[me]

    def take_meta(d, c):
        meta_copy(d).wait()
        return c

    lax.fori_loop(1, nv, take_meta, 0)

    def done_rec(s, c):
        rec_copy(s).wait_send()
        return c

    lax.fori_loop(1, views, done_rec, 0)

    target, weights = landing_facts(meta_recv[...].reshape(nv, 128), 1)
    place_t = (lane_of.astype(f32) == target).astype(f32)
    placed = place_t.T[0:TROWS, :].astype(bf16)
    counted = jnp.dot(
        placed, jnp.broadcast_to(weights, (landing, depth)).astype(bf16), preferred_element_type=f32
    )

    def take_data(d, c):
        data_copy(d).wait()
        return c

    lax.fori_loop(1, nv, take_data, 0)
    summed = onehot_dot(placed, split3(data_recv[:, :slab, :].reshape(landing, depth)))
    joined = (1.0 + summed) / (1.0 + counted)
    edges = jnp.sum(data_recv[:, slab:, :], axis=0)
    edges = (1.0 + edges[0:2]) / (1.0 + edges[2:4])
    low_line = jnp.where(me > 0, edges[0:1], 0.0)
    high_line = jnp.where(me < nv - 1, edges[1:2], 0.0)

    lane = lax.broadcasted_iota(jnp.int32, (TROWS, depth), 1)
    line = lax.broadcasted_iota(jnp.int32, (TROWS, depth), 0)

    def flux(neighbor):
        change = neighbor - joined
        return change / (1.0 + change * change)

    right = jnp.where(lane == depth - 1, 0.0, pltpu.roll(joined, depth - 1, 1))
    left = jnp.where(lane == 0, 0.0, pltpu.roll(joined, 1, 1))
    along_depth = flux(right) + flux(left)
    after = pltpu.roll(joined, TROWS - 1, 0)
    before = pltpu.roll(joined, 1, 0)
    after = jnp.where(line == TROWS - 1, high_line, after)
    before = jnp.where(line == 0, low_line, before)
    smooth_ref[...] = joined + smooth_rate * (flux(after) + flux(before) + along_depth)


def on_device(
    estimate,
    measured,
    kernel_z,
    kernel_x,
    kernel_y,
    background,
    relax,
    owner,
    source_offset,
    tile_offset,
    feather,
):
    nv = lax.axis_size("view")
    views, rank, bx, _ = kernel_x.shape
    by = kernel_y.shape[-1]
    rows, depth = estimate.shape
    srows = feather.shape[1]
    listed = owner.shape[0]
    slab = CAP * srows
    landing = nv * slab

    col = np.arange(rank * rows)
    sel_x = col[None, :] // by == np.arange(rank * bx)[:, None]
    sel_y = (col // rows * by + col % by)[None, :] == np.arange(rank * by)[:, None]
    sel_x = jnp.asarray(sel_x.reshape(rank, bx, -1).astype(np.float32), bf16)
    sel_y = jnp.asarray(sel_y.reshape(rank, by, -1).astype(np.float32), bf16)

    vmem = pl.BlockSpec(memory_space=pltpu.VMEM)
    anym = pl.BlockSpec(memory_space=pl.ANY)
    dma = pltpu.SemaphoreType.DMA
    return pl.pallas_call(
        functools.partial(kernel, nv, views, bx, by, srows),
        out_shape=(
            jax.ShapeDtypeStruct((rows, depth), f32),
            jax.ShapeDtypeStruct((TROWS, depth), f32),
        ),
        in_specs=[vmem, anym, anym] + [vmem] * 10,
        out_specs=(vmem, vmem),
        scratch_shapes=[
            pltpu.VMEM((views, rows, depth), bf16),
            pltpu.VMEM(kernel_z.shape, bf16),
            pltpu.VMEM((bx * views, rank * rows), f32),
            pltpu.VMEM((views * by, rank * rows), f32),
            pltpu.VMEM((2, rows, rank * rows), bf16),
            pltpu.VMEM((2, rank * rows, rows), bf16),
            pltpu.VMEM((2, rows, depth), f32),
            pltpu.VMEM((nv, 1, 128), f32),
            pltpu.VMEM((nv, 1, 128), f32),
            pltpu.VMEM((landing, rows), bf16),
            pltpu.VMEM((nv * EDGE, rows), bf16),
            pltpu.VMEM((nv * EDGE, depth), f32),
            pltpu.VMEM((nv, slab + EDGE, depth), f32),
            pltpu.VMEM((nv, slab + EDGE, depth), f32),
            dma((views,)),
            dma((views,)),
            dma,
            dma((nv,)),
            dma((nv,)),
            dma((nv,)),
            dma((nv,)),
        ],
        compiler_params=pltpu.CompilerParams(collective_id=0, has_side_effects=True),
    )(
        estimate,
        measured,
        kernel_z,
        kernel_x.transpose(1, 2, 0, 3),
        kernel_y,
        sel_x,
        sel_y,
        background.reshape(1, views),
        relax.reshape(1, views),
        owner.reshape(1, listed),
        source_offset.reshape(1, listed),
        tile_offset.reshape(1, listed),
        feather.T,
    )


def solution(mesh):
    return jax.shard_map(
        on_device,
        mesh=mesh,
        in_specs=(
            P(("groups", "view"), None),
            P(("groups", "view"), None, None),
            P(),
            P(),
            P(),
            P(),
            P(),
            P(("groups", "view"), None),
            P(("groups", "view")),
            P(("groups", "view")),
            P(("groups", "view"), None),
        ),
        out_specs=(P(("groups", "view"), None), P(("groups", "view"), None)),
        check_vma=False,
    )
```

```python
import functools

import jax
import jax.numpy as jnp
import numpy as np
from jax import lax
from jax.experimental import pallas as pl
from jax.experimental.pallas import tpu as pltpu
from jax.sharding import PartitionSpec as P

CAP = 2
FIELDS = 16
EDGE = 8
AHEAD = 4
TROWS = 64
smooth_rate = 0.24

f32 = jnp.float32
bf16 = jnp.bfloat16


def split3(x):
    hi = x.astype(bf16)
    rest = x - hi.astype(f32)
    mid = rest.astype(bf16)
    low = (rest - mid.astype(f32)).astype(bf16)
    return hi, mid, low


def onehot_dot(onehot, parts):
    total = None
    for part in reversed(parts):
        term = jnp.dot(onehot, part, preferred_element_type=f32)
        total = term if total is None else total + term
    return total


def kernel(
    nv,
    views,
    bx,
    by,
    srows,
    est_ref,
    meas_hbm,
    kz_hbm,
    kx_ref,
    ky_ref,
    sel_x_ref,
    sel_y_ref,
    back_ref,
    relax_ref,
    owner_ref,
    source_ref,
    tile_ref,
    feather_ref,
    refined_ref,
    smooth_ref,
    rec,
    kz,
    lanes_x,
    lanes_y,
    kron,
    kron_t,
    logws,
    meta_send,
    meta_recv,
    gather,
    edge_lines,
    edge_counts,
    data_send,
    data_recv,
    rec_send_sem,
    rec_recv_sem,
    kz_sem,
    meta_send_sem,
    meta_recv_sem,
    data_send_sem,
    data_recv_sem,
):
    me = lax.axis_index("view")
    rows, depth = est_ref.shape
    rank = kz.shape[1]
    listed = owner_ref.shape[1]
    slab = CAP * srows
    landing = nv * slab

    barrier = pltpu.get_barrier_semaphore()

    def greet(d, c):
        pl.semaphore_signal(barrier, inc=1, device_id={"view": lax.rem(me + d, nv)})
        return c

    lax.fori_loop(1, nv, greet, 0)

    own_rec = pltpu.make_async_copy(meas_hbm.at[0], rec.at[0], rec_recv_sem.at[0])
    own_rec.start()
    kz_copy = pltpu.make_async_copy(kz_hbm, kz, kz_sem)
    kz_copy.start()

    def rec_copy(s):
        return pltpu.make_async_remote_copy(
            src_ref=meas_hbm.at[s],
            dst_ref=rec.at[s],
            send_sem=rec_send_sem.at[s],
            recv_sem=rec_recv_sem.at[s],
            device_id={"view": lax.rem(me - s + nv, nv)},
        )

    def peer_copy(src, dst, send_sem, recv_sem, d):
        peer = lax.rem(me + d, nv)
        return pltpu.make_async_remote_copy(
            src_ref=src.at[peer],
            dst_ref=dst.at[me],
            send_sem=send_sem.at[d],
            recv_sem=recv_sem.at[d],
            device_id={"view": peer},
        )

    def meta_copy(d):
        return peer_copy(meta_send, meta_recv, meta_send_sem, meta_recv_sem, d)

    def data_copy(d):
        return peer_copy(data_send, data_recv, data_send_sem, data_recv_sem, d)

    pl.semaphore_wait(barrier, nv - 1)

    def send_rec(s, c):
        rec_copy(s).start()
        return c

    lax.fori_loop(1, AHEAD, send_rec, 0)

    spread_x = spread_y = None
    for r in range(rank):
        part_x = jnp.dot(kx_ref[r].reshape(bx * views, bx), sel_x_ref[r], preferred_element_type=f32)
        part_y = jnp.dot(ky_ref[:, r].reshape(views * by, by), sel_y_ref[r], preferred_element_type=f32)
        spread_x = part_x if spread_x is None else spread_x + part_x
        spread_y = part_y if spread_y is None else spread_y + part_y
    lanes_x[...] = spread_x
    lanes_y[...] = spread_y

    own_row = owner_ref[...].astype(f32)
    if listed < 128:
        own_row = jnp.concatenate([own_row, jnp.full((1, 128 - listed), -1.0, f32)], axis=1)
    own_wide = jnp.broadcast_to(own_row, (128, 128)).T
    same = (own_wide == own_row).astype(f32)
    ia = lax.broadcasted_iota(jnp.int32, (128, 128), 0)
    ib = lax.broadcasted_iota(jnp.int32, (128, 128), 1)
    earlier = jnp.where(ia < ib, same, 0.0)
    rank_row = jnp.sum(earlier, axis=0, keepdims=True)
    slot_row = own_row * CAP + rank_row
    fields = jnp.concatenate(
        [
            source_ref[...].astype(f32),
            tile_ref[...].astype(f32),
            jnp.ones((1, listed), f32),
            feather_ref[...].astype(f32),
            jnp.zeros((FIELDS - 3 - srows, listed), f32),
        ],
        axis=0,
    ).astype(bf16)
    slot_ids = lax.broadcasted_iota(jnp.int32, (nv, 128), 0).astype(f32) * CAP
    facts = []
    for c in range(CAP):
        pick = (slot_ids + c == slot_row).astype(f32)[:, :listed].astype(bf16)
        facts.append(
            lax.dot_general(pick, fields, (((1,), (1,)), ((), ())), preferred_element_type=f32)
        )
    facts.append(jnp.zeros((nv, 128 - CAP * FIELDS), f32))
    facts = jnp.concatenate(facts, axis=1)
    meta_send[...] = facts.reshape(nv, 1, 128)

    def send_meta(d, c):
        meta_copy(d).start()
        return c

    lax.fori_loop(1, nv, send_meta, 0)

    row_id = lax.broadcasted_iota(jnp.int32, (landing, 128), 0)
    lane_of = lax.broadcasted_iota(jnp.int32, (landing, 128), 1)
    q_of_row = lax.rem(row_id, srows)
    first_lane = lax.rem(row_id, slab) // srows * FIELDS
    spread_rows = (
        lax.broadcasted_iota(jnp.int32, (landing, nv), 0) // slab
        == lax.broadcasted_iota(jnp.int32, (landing, nv), 1)
    ).astype(f32).astype(bf16)

    def landing_facts(table, line_lane):
        wide = jnp.dot(spread_rows, table.astype(bf16), preferred_element_type=f32)

        def column(lane):
            return jnp.sum(jnp.where(lane_of == lane, wide, 0.0), axis=1, keepdims=True)

        line = column(first_lane + line_lane) + q_of_row[:, 0:1].astype(f32)
        return line + (column(first_lane + 2) - 1.0) * 4096.0, column(first_lane + 3 + q_of_row)

    view0 = lax.rem(me, views)

    def expand(view, slot):
        y_part = lanes_y[pl.ds(pl.multiple_of(view * by, by), by), :]
        for x in range(bx):
            x_part = lanes_x[pl.ds(x * views + view, 1), :]
            kron[slot, x * by : (x + 1) * by, :] = (x_part * y_part).astype(bf16)

    def weigh(view, slot):
        kron_t[slot] = kron[slot].T
        halves = None
        for r in range(rank):
            column = jnp.sum(kz[view, r].astype(f32), axis=0, keepdims=True)
            hi = column.astype(bf16).astype(f32)
            both = jnp.concatenate([hi, column - hi], axis=1)
            both = jnp.broadcast_to(both, (rows, 2 * depth)).astype(bf16)
            part = jnp.dot(
                kron_t[slot, r * rows : (r + 1) * rows, :], both, preferred_element_type=f32
            )
            halves = part if halves is None else halves + part
        logws[slot] = jnp.log(halves[:, :depth] + halves[:, depth:])

    def scalar(ref, view):
        lane = lax.broadcasted_iota(jnp.int32, (1, views), 1)
        return jnp.sum(jnp.where(lane == view, ref[...].astype(f32), 0.0), axis=1, keepdims=True)

    expand(view0, 0)
    refined_ref[...] = est_ref[...]
    kz_copy.wait()
    weigh(view0, 0)
    source, weight = landing_facts(facts, 0)
    target, _ = landing_facts(facts, 1)
    lane_rows = lax.broadcasted_iota(jnp.int32, (landing, rows), 1).astype(f32)
    weighted = jnp.where(lane_rows == source, weight, 0.0).astype(bf16)
    gather[...] = weighted
    target_row = jnp.broadcast_to(target, (landing, 128)).T[0:1, :]
    edge_row = lax.broadcasted_iota(jnp.int32, (nv * EDGE, landing), 0)
    edge_kind = lax.rem(edge_row, EDGE)
    side = lax.rem(edge_kind, 2)
    wanted = edge_row // EDGE + 2 * side - 1
    lane_tile = lax.broadcasted_iota(jnp.int32, (nv * EDGE, landing), 1) // slab
    near = jnp.where(side == 0, float(TROWS - 1), 0.0)
    member = ((lane_tile == wanted).astype(f32) * (target_row == near).astype(f32)).astype(bf16)
    kind = lax.rem(lax.broadcasted_iota(jnp.int32, (nv * EDGE, 1), 0), EDGE)
    from_lines = jnp.dot(member, weighted, preferred_element_type=f32)
    edge_lines[...] = jnp.where(kind < 2, from_lines, 0.0).astype(bf16)
    from_weights = jnp.dot(
        member, jnp.broadcast_to(weight, (landing, depth)).astype(bf16), preferred_element_type=f32
    )
    edge_counts[...] = jnp.where((kind >= 2) & (kind < 4), from_weights, 0.0)
    own_rec.wait()

    def stop(s, c):
        @pl.when(s > 0)
        def _():
            rec_copy(s).wait_recv()

        @pl.when(s + AHEAD < views)
        def _():
            rec_copy(s + AHEAD).start()

        slot = lax.rem(s, 2)
        view = lax.rem(me + s, views)
        e = refined_ref[...]
        zeta = kz[view]
        low = e.astype(bf16)
        along = [
            lax.dot_general(
                low, zeta[r], (((1,), (1,)), ((), ())), preferred_element_type=f32
            ).astype(bf16)
            for r in range(rank)
        ]
        forward = jnp.dot(kron[slot], jnp.concatenate(along, axis=0), preferred_element_type=f32)
        ratio = (rec[s].astype(f32) / (forward + scalar(back_ref, view))).astype(bf16)
        back = [
            jnp.dot(ratio, zeta[r], preferred_element_type=f32).astype(bf16) for r in range(rank)
        ]
        adjoint = None
        for r in range(rank):
            part = jnp.dot(
                kron_t[slot, r * rows : (r + 1) * rows, :], back[r], preferred_element_type=f32
            )
            adjoint = part if adjoint is None else adjoint + part
        refined_ref[...] = e * jnp.exp(scalar(relax_ref, view) * (jnp.log(adjoint) - logws[slot]))
        following = lax.rem(view + 1, views)
        expand(following, 1 - slot)
        weigh(following, 1 - slot)
        return c

    lax.fori_loop(0, views, stop, 0)

    parts = split3(refined_ref[...])
    data_send[:, :slab, :] = onehot_dot(gather[...], parts).reshape(nv, slab, depth)
    data_send[:, slab:, :] = (onehot_dot(edge_lines[...], parts) + edge_counts[...]).reshape(
        nv, EDGE, depth
    )

    def send_data(d, c):
        data_copy(d).start()
        return c

    lax.fori_loop(1, nv, send_data, 0)
    data_recv[me] = data_send[me]
    meta_recv[me] = meta_send[me]

    def take_meta(d, c):
        meta_copy(d).wait()
        return c

    lax.fori_loop(1, nv, take_meta, 0)

    def done_rec(s, c):
        rec_copy(s).wait_send()
        return c

    lax.fori_loop(1, views, done_rec, 0)

    target, weights = landing_facts(meta_recv[...].reshape(nv, 128), 1)
    place_t = (lane_of.astype(f32) == target).astype(f32)
    placed = place_t.T[0:TROWS, :].astype(bf16)
    counted = jnp.dot(
        placed, jnp.broadcast_to(weights, (landing, depth)).astype(bf16), preferred_element_type=f32
    )

    def take_data(d, c):
        data_copy(d).wait()
        return c

    lax.fori_loop(1, nv, take_data, 0)
    summed = onehot_dot(placed, split3(data_recv[:, :slab, :].reshape(landing, depth)))
    joined = (1.0 + summed) / (1.0 + counted)
    edges = jnp.sum(data_recv[:, slab:, :], axis=0)
    edges = (1.0 + edges[0:2]) / (1.0 + edges[2:4])
    low_line = jnp.where(me > 0, edges[0:1], 0.0)
    high_line = jnp.where(me < nv - 1, edges[1:2], 0.0)

    lane = lax.broadcasted_iota(jnp.int32, (TROWS, depth), 1)
    line = lax.broadcasted_iota(jnp.int32, (TROWS, depth), 0)

    def flux(neighbor):
        change = neighbor - joined
        return change / (1.0 + change * change)

    right = jnp.where(lane == depth - 1, 0.0, pltpu.roll(joined, depth - 1, 1))
    left = jnp.where(lane == 0, 0.0, pltpu.roll(joined, 1, 1))
    along_depth = flux(right) + flux(left)
    after = pltpu.roll(joined, TROWS - 1, 0)
    before = pltpu.roll(joined, 1, 0)
    after = jnp.where(line == TROWS - 1, high_line, after)
    before = jnp.where(line == 0, low_line, before)
    smooth_ref[...] = joined + smooth_rate * (flux(after) + flux(before) + along_depth)


def on_device(
    estimate,
    measured,
    kernel_z,
    kernel_x,
    kernel_y,
    background,
    relax,
    owner,
    source_offset,
    tile_offset,
    feather,
):
    nv = lax.axis_size("view")
    views, rank, bx, _ = kernel_x.shape
    by = kernel_y.shape[-1]
    rows, depth = estimate.shape
    srows = feather.shape[1]
    listed = owner.shape[0]
    slab = CAP * srows
    landing = nv * slab

    col = np.arange(rank * rows)
    sel_x = col[None, :] // by == np.arange(rank * bx)[:, None]
    sel_y = (col // rows * by + col % by)[None, :] == np.arange(rank * by)[:, None]
    sel_x = jnp.asarray(sel_x.reshape(rank, bx, -1).astype(np.float32), bf16)
    sel_y = jnp.asarray(sel_y.reshape(rank, by, -1).astype(np.float32), bf16)

    vmem = pl.BlockSpec(memory_space=pltpu.VMEM)
    anym = pl.BlockSpec(memory_space=pl.ANY)
    dma = pltpu.SemaphoreType.DMA
    return pl.pallas_call(
        functools.partial(kernel, nv, views, bx, by, srows),
        out_shape=(
            pltpu.VMEM((rows, depth), f32),
            pltpu.VMEM((TROWS, depth), f32),
        ),
        in_specs=[vmem, anym, anym] + [vmem] * 10,
        out_specs=(vmem, vmem),
        scratch_shapes=[
            pltpu.VMEM((views, rows, depth), bf16),
            pltpu.VMEM(kernel_z.shape, bf16),
            pltpu.VMEM((bx * views, rank * rows), f32),
            pltpu.VMEM((views * by, rank * rows), f32),
            pltpu.VMEM((2, rows, rank * rows), bf16),
            pltpu.VMEM((2, rank * rows, rows), bf16),
            pltpu.VMEM((2, rows, depth), f32),
            pltpu.VMEM((nv, 1, 128), f32),
            pltpu.VMEM((nv, 1, 128), f32),
            pltpu.VMEM((landing, rows), bf16),
            pltpu.VMEM((nv * EDGE, rows), bf16),
            pltpu.VMEM((nv * EDGE, depth), f32),
            pltpu.VMEM((nv, slab + EDGE, depth), f32),
            pltpu.VMEM((nv, slab + EDGE, depth), f32),
            dma((views,)),
            dma((views,)),
            dma,
            dma((nv,)),
            dma((nv,)),
            dma((nv,)),
            dma((nv,)),
        ],
        compiler_params=pltpu.CompilerParams(collective_id=0, has_side_effects=True),
    )(
        estimate,
        measured,
        kernel_z,
        kernel_x.transpose(1, 2, 0, 3),
        kernel_y,
        sel_x,
        sel_y,
        background.reshape(1, views),
        relax.reshape(1, views),
        owner.reshape(1, listed),
        source_offset.reshape(1, listed),
        tile_offset.reshape(1, listed),
        feather.T,
    )


def solution(mesh):
    return jax.shard_map(
        on_device,
        mesh=mesh,
        in_specs=(
            P(("groups", "view"), None),
            P(("groups", "view"), None, None),
            P(),
            P(),
            P(),
            P(),
            P(),
            P(("groups", "view"), None),
            P(("groups", "view")),
            P(("groups", "view")),
            P(("groups", "view"), None),
        ),
        out_specs=(P(("groups", "view"), None), P(("groups", "view"), None)),
        check_vma=False,
    )
```
